32 devices in a mesh: fsdp: 4 (over z), tensor: 8 (over y, x, core).
Axes of the slice: x: 2, y: 2, z: 4, core: 2. Of those that a mesh axis runs over, the one named last changes fastest.
Arguments:
- hidden_in: bfloat16 [2048, 1024], P('fsdp'), may hold values from -6 to 6
- out_cotangent: float32 [2048, 1024], P('fsdp'), may hold values from -0.25 to 0.25
- qkv_weight: bfloat16 [2, 1024, 16, 192], P(None, 'fsdp', 'tensor'), may hold values from -1 to 1
- query_value_bias: bfloat16 [2, 16, 128], P(None, 'tensor', 'fsdp'), may hold values from -3 to 3
- attn_out_weight: bfloat16 [2, 16, 64, 1024], P(None, 'tensor', None, 'fsdp'), may hold values from -0.75 to 0.75
- up_weight: bfloat16 [2, 1024, 4096], P(None, 'fsdp', 'tensor'), may hold values from -0.1875 to 0.1875
- up_bias: bfloat16 [2, 4096], P(None, ('tensor', 'fsdp')), may hold values from -3 to 3
- down_weight: bfloat16 [2, 4096, 1024], P(None, 'tensor', 'fsdp'), may hold values from -0.09375 to 0.09375
- block_bias: bfloat16 [2, 2, 1024], P(None, None, 'fsdp'), may hold values from -2 to 2
- norm_gain: bfloat16 [2, 2, 1024], P(None, None, 'fsdp'), may hold values from 0.099609375 to 1.8984375
- norm_shift: bfloat16 [2, 2, 1024], P(None, None, 'fsdp'), may hold values from -2 to 2
Outputs:
- activations: float32 [2048, 1024], P('fsdp')
- input_grad: float32 [2048, 1024], P('fsdp')
- grad_qkv_weight: float32 [2, 1024, 16, 192], P(None, 'fsdp', 'tensor')
- grad_query_value_bias: float32 [2, 16, 128], P(None, 'tensor', 'fsdp')
- grad_attn_out_weight: float32 [2, 16, 64, 1024], P(None, 'tensor', None, 'fsdp')
- grad_up_weight: float32 [2, 1024, 4096], P(None, 'fsdp', 'tensor')
- grad_up_bias: float32 [2, 4096], P(None, ('tensor', 'fsdp'))
- grad_down_weight: float32 [2, 4096, 1024], P(None, 'tensor', 'fsdp')
- grad_block_bias: float32 [2, 2, 1024], P(None, None, 'fsdp')
- grad_norm_gain: float32 [2, 2, 1024], P(None, None, 'fsdp')
- grad_norm_shift: float32 [2, 2, 1024], P(None, None, 'fsdp')
The draws below stay inside these ranges and needn't reach their ends.
All inputs are finite; a program needn't handle non-finite values.
Results may differ from the reference program's by a relative error of at most 0.02.
Values may be sent and summed in bfloat16 or wider, within the bound.
No kernel may reach another device: no remote copies, remote signals or barrier semaphores. Data moves between devices by JAX's collectives and lax.ppermute only.
A program may use at most 128 MiB of HBM per device.

```python
import math
import jax
import jax.numpy as jnp
from jax import lax

D = 1024
HEADS = 16
HD = 64
FF = 4096
SEQ = 512
LAYERS = 2
TOKENS = 2048


def draw_hidden_in(key, part):
    array_shape = (TOKENS, D)
    values = jnp.clip(jax.random.normal(key, array_shape, jnp.float32), -6.0, 6.0)
    return values.astype(jnp.bfloat16)


def draw_qkv_weight(key, part):
    query_seed, key_seed, value_seed = jax.random.split(key, 3)
    array_shape = (LAYERS, D, HEADS, HD)
    query_part = jax.random.normal(query_seed, array_shape, jnp.float32)
    key_part = jax.random.normal(key_seed, array_shape, jnp.float32)
    value_part = jax.random.normal(value_seed, array_shape, jnp.float32)
    joined = jnp.concatenate([query_part, key_part, value_part], axis=-1)
    return (jnp.clip(joined, -5.0, 5.0) * (1.0 / math.sqrt(D))).astype(jnp.bfloat16)


def shard_levels(key, extent, pieces, least, largest):
    factor_of, own = 1.0, jax.random.fold_in(key, 6)
    for dim, blocks in pieces:
        steps = jnp.exp(jax.random.uniform(jax.random.fold_in(own, dim), (blocks,), jnp.float32, least / len(pieces), largest / len(pieces)))
        factor_of = factor_of * jnp.repeat(steps, extent[dim] // blocks).reshape([-1 if axis == dim else 1 for axis in range(len(extent))])
    return factor_of


def gaussian(key, dims, width, limit, shards=(), held_as=jnp.bfloat16):
    entries = jax.random.normal(key, dims, jnp.float32) * width
    if len(shards) > 0:
        entries = shard_levels(key, dims, shards, -0.22, 0.18) * entries
    return jnp.clip(entries, min=-limit, max=limit).astype(held_as)


def setup_inputs(seed: int = 0) -> dict:
    key_list = jax.random.split(jax.random.key(seed), 12)
    hidden_in = draw_hidden_in(jax.random.fold_in(key_list[11], 71), 0)
    out_cotangent = gaussian(key_list[1], (TOKENS, D), (2 * TOKENS ** -0.5), 0.25, ((0, 4),), jnp.float32)
    qkv_weight = draw_qkv_weight(jax.random.fold_in(key_list[11], 71), 0)
    query_value_bias = gaussian(key_list[3], (LAYERS, HEADS, 2 * HD), 0.5, 3.0, ((1, 8), (2, 4)))
    attn_out_weight = gaussian(key_list[4], (LAYERS, HEADS, HD, D), HD ** -0.5, 0.75, ((1, 8), (3, 4)))
    up_weight = gaussian(key_list[5], (LAYERS, D, FF), D ** -0.5, 0.1875, ((1, 4), (2, 8)))
    up_bias = gaussian(key_list[6], (LAYERS, FF), 0.5, 3.0, ((1, 32),))
    down_weight = gaussian(key_list[7], (LAYERS, FF, D), FF ** -0.5, 0.09375, ((1, 8), (2, 4)))
    block_bias = gaussian(key_list[8], (LAYERS, 2, D), 0.3, 2.0, ((2, 4),))
    norm_gain = jnp.clip(1.0 + 0.18 * jax.random.normal(key_list[9], (LAYERS, 2, D), jnp.float32), 0.099609375, 1.8984375).astype(jnp.bfloat16)
    norm_shift = gaussian(key_list[10], (LAYERS, 2, D), 0.3, 2.0, ((2, 4),))
    return dict(hidden_in=hidden_in, out_cotangent=out_cotangent, qkv_weight=qkv_weight, query_value_bias=query_value_bias, attn_out_weight=attn_out_weight, up_weight=up_weight, up_bias=up_bias, down_weight=down_weight, block_bias=block_bias, norm_gain=norm_gain, norm_shift=norm_shift)


eps_norm = 1e-05
root_half = 0.7071067811865476
inv_root_two_pi = 0.3989422804014327
contract_rows = (((0,), (0,)), ((), ()))
contract_cols = (((1,), (1,)), ((), ()))

def gelu_value(pre_act):
    return 0.5 * pre_act * (1.0 + lax.erf(pre_act * root_half))

def gelu_slope(pre_act):
    return 0.5 * (1.0 + lax.erf(pre_act * root_half)) + pre_act * inv_root_two_pi * jnp.exp(-0.5 * pre_act * pre_act)

def normalize(summed, gain_vec, offset_vec):
    center = summed - lax.optimization_barrier(jnp.mean(summed, axis=-1, keepdims=True))
    scaled = lax.rsqrt(lax.optimization_barrier(jnp.mean(center * center, axis=-1, keepdims=True)) + eps_norm)
    normed = center * scaled
    return (normed * gain_vec + offset_vec, normed, scaled)

def normalize_back(upstream, normed, scaled, gain_vec):
    weighted = upstream * gain_vec
    return scaled * (weighted - lax.optimization_barrier(jnp.mean(weighted, axis=-1, keepdims=True)) - normed * lax.optimization_barrier(jnp.mean(weighted * normed, axis=-1, keepdims=True)))

def group_sum(left, right):
    return jnp.dot(left, right, preferred_element_type=jnp.float32)

def attend_one(trio):
    query_rows, key_rows, value_rows = trio
    scores = jnp.einsum('qhd,khd->hqk', query_rows.astype(jnp.float32), key_rows.astype(jnp.float32)) * HD ** (-0.5)
    row_max = lax.optimization_barrier(jnp.max(scores, axis=-1, keepdims=True))
    logsum = row_max + jnp.log(lax.optimization_barrier(jnp.sum(jnp.exp(scores - row_max), axis=-1, keepdims=True)))
    attn_probs = lax.optimization_barrier(jnp.exp(scores - logsum).astype(jnp.bfloat16))
    context = jnp.einsum('hqk,khd->qhd', attn_probs.astype(jnp.float32), value_rows.astype(jnp.float32))
    return (context.astype(jnp.bfloat16), logsum)

def attend_back_one(group):
    query_rows, key_rows, value_rows, logsum, grad_context = group
    scale_factor = HD ** (-0.5)
    scores = jnp.einsum('qhd,khd->hqk', query_rows.astype(jnp.float32), key_rows.astype(jnp.float32)) * scale_factor
    attn_probs = jnp.exp(scores - logsum)
    low_probs = lax.optimization_barrier(attn_probs.astype(jnp.bfloat16)).astype(jnp.float32)
    context_wide = grad_context.astype(jnp.float32)
    grad_value = jnp.einsum('hqk,qhd->khd', low_probs, context_wide)
    grad_probs = jnp.einsum('qhd,khd->hqk', context_wide, value_rows.astype(jnp.float32))
    inner_sum = lax.optimization_barrier(jnp.sum(attn_probs * grad_probs, axis=-1, keepdims=True))
    grad_scores = lax.optimization_barrier((attn_probs * (grad_probs - inner_sum)).astype(jnp.bfloat16)).astype(jnp.float32)
    grad_query = jnp.einsum('hqk,khd->qhd', grad_scores, key_rows.astype(jnp.float32)) * scale_factor
    grad_key = jnp.einsum('hqk,qhd->khd', grad_scores, query_rows.astype(jnp.float32)) * scale_factor
    return (grad_query, grad_key, grad_value)

def forward_layer(stream_rows, low_full, params):
    weight_qkv, bias_qv, weight_out, weight_up, bias_up, weight_down, bias_block, gain_vec, offset_vec = params
    row_count = low_full.shape[0]
    projected = jnp.dot(low_full, weight_qkv.reshape(D, HEADS * 3 * HD), preferred_element_type=jnp.float32).reshape(row_count, HEADS, 3 * HD)
    bias_wide = bias_qv.astype(jnp.float32)
    blocks = (row_count // SEQ, SEQ, HEADS, HD)
    query_rows = (projected[..., :HD] + bias_wide[:, :HD]).astype(jnp.bfloat16).reshape(blocks)
    key_rows = projected[..., HD:2 * HD].astype(jnp.bfloat16).reshape(blocks)
    value_rows = (projected[..., 2 * HD:] + bias_wide[:, HD:]).astype(jnp.bfloat16).reshape(blocks)
    context, logsum = lax.map(attend_one, (query_rows, key_rows, value_rows))
    flat_context = context.reshape(row_count, HEADS * HD)
    summed_one = stream_rows + group_sum(flat_context, weight_out.reshape(HEADS * HD, D)) + bias_block[0].astype(jnp.float32)
    first_norm, normed_one, scale_one = normalize(summed_one, gain_vec[0].astype(jnp.float32), offset_vec[0].astype(jnp.float32))
    low_norm = first_norm.astype(jnp.bfloat16)
    pre_act = jnp.dot(low_norm, weight_up, preferred_element_type=jnp.float32) + bias_up.astype(jnp.float32)
    activated = gelu_value(pre_act).astype(jnp.bfloat16)
    summed_two = first_norm + group_sum(activated, weight_down) + bias_block[1].astype(jnp.float32)
    output, normed_two, scale_two = normalize(summed_two, gain_vec[1].astype(jnp.float32), offset_vec[1].astype(jnp.float32))
    stored = (low_full, query_rows, key_rows, value_rows, logsum, context, normed_one, scale_one, low_norm, pre_act, activated, normed_two, scale_two)
    return (output, stored)

def backward_layer(grad_rows, stored, params):
    weight_qkv, bias_qv, weight_out, weight_up, bias_up, weight_down, bias_block, gain_vec, offset_vec = params
    low_full, query_rows, key_rows, value_rows, logsum, context, normed_one, scale_one, low_norm, pre_act, activated, normed_two, scale_two = stored
    row_count = low_full.shape[0]
    grad_two = normalize_back(grad_rows, normed_two, scale_two, gain_vec[1].astype(jnp.float32))
    low_two = grad_two.astype(jnp.bfloat16)
    grad_down = lax.dot_general(activated, low_two, contract_rows, preferred_element_type=jnp.float32)
    grad_pre = lax.dot_general(low_two, weight_down, contract_cols, preferred_element_type=jnp.float32) * gelu_slope(pre_act)
    low_pre = grad_pre.astype(jnp.bfloat16)
    grad_up = lax.dot_general(low_norm, low_pre, contract_rows, preferred_element_type=jnp.float32)
    grad_up_bias = lax.optimization_barrier(jnp.sum(grad_pre, axis=0))
    grad_first = grad_two + group_sum(low_pre, weight_up.T)
    grad_one = normalize_back(grad_first, normed_one, scale_one, gain_vec[0].astype(jnp.float32))
    low_one = grad_one.astype(jnp.bfloat16)
    flat_context = context.reshape(row_count, HEADS * HD)
    grad_out_w = lax.dot_general(flat_context, low_one, contract_rows, preferred_element_type=jnp.float32).reshape(HEADS, HD, D)
    grad_context = lax.dot_general(low_one, weight_out.reshape(HEADS * HD, D), contract_cols, preferred_element_type=jnp.float32)
    grad_context = grad_context.astype(jnp.bfloat16).reshape(query_rows.shape)
    grad_query, grad_key, grad_value = lax.map(attend_back_one, (query_rows, key_rows, value_rows, logsum, grad_context))
    low_mixed = jnp.concatenate([grad_query, grad_key, grad_value], axis=-1).astype(jnp.bfloat16).reshape(row_count, HEADS * 3 * HD)
    grad_qkv = lax.dot_general(low_full, low_mixed, contract_rows, preferred_element_type=jnp.float32).reshape(D, HEADS, 3 * HD)
    grad_qv = jnp.concatenate([lax.optimization_barrier(jnp.sum(grad_query, axis=(0, 1))), lax.optimization_barrier(jnp.sum(grad_value, axis=(0, 1)))], axis=-1)
    grad_in = grad_one + group_sum(low_mixed, weight_qkv.reshape(D, HEADS * 3 * HD).T)
    grad_block = jnp.stack([lax.optimization_barrier(jnp.sum(grad_one, axis=0)), lax.optimization_barrier(jnp.sum(grad_two, axis=0))])
    grad_gain = jnp.stack([lax.optimization_barrier(jnp.sum(grad_first * normed_one, axis=0)), lax.optimization_barrier(jnp.sum(grad_rows * normed_two, axis=0))])
    grad_offset = jnp.stack([lax.optimization_barrier(jnp.sum(grad_first, axis=0)), lax.optimization_barrier(jnp.sum(grad_rows, axis=0))])
    return (grad_in, (grad_qkv, grad_qv, grad_out_w, grad_up, grad_up_bias, grad_down, grad_block, grad_gain, grad_offset))

def reference(hidden_in, out_cotangent, qkv_weight, query_value_bias, attn_out_weight, up_weight, up_bias, down_weight, block_bias, norm_gain, norm_shift):
    stacked = (qkv_weight, query_value_bias, attn_out_weight, up_weight, up_bias, down_weight, block_bias, norm_gain, norm_shift)
    stream_rows = hidden_in.astype(jnp.float32)
    low_full = hidden_in
    kept_stores = []
    for layer_index in range(LAYERS):
        params = tuple((member[layer_index] for member in stacked))
        stream_rows, stored = forward_layer(stream_rows, low_full, params)
        kept_stores.append(stored)
        low_full = stream_rows.astype(jnp.bfloat16)
    grad_rows = out_cotangent
    layer_grads = [None] * LAYERS
    for layer_index in reversed(range(LAYERS)):
        params = tuple((member[layer_index] for member in stacked))
        grad_rows, layer_grads[layer_index] = backward_layer(grad_rows, kept_stores[layer_index], params)
    outputs = tuple((jnp.stack([layer_set[member_index] for layer_set in layer_grads]) for member_index in range(9)))
    return (stream_rows, grad_rows, outputs[0], outputs[1], outputs[2], outputs[3], outputs[4], outputs[5], outputs[6], outputs[7], outputs[8])
```

```python
import jax
import jax.numpy as jnp
from jax import lax
from jax.sharding import PartitionSpec as P

SEQ = 512

eps_norm = 1e-05
root_half = 0.7071067811865476
inv_root_two_pi = 0.3989422804014327
contract_rows = (((0,), (0,)), ((), ()))
contract_cols = (((1,), (1,)), ((), ()))
f32 = jnp.float32
bf16 = jnp.bfloat16


def gelu_both(pre_act):
    half = 0.5 * (1.0 + lax.erf(pre_act * root_half))
    return half


def normalize(summed, gain_vec, offset_vec):
    center = summed - jnp.mean(summed, axis=-1, keepdims=True)
    scaled = lax.rsqrt(jnp.mean(center * center, axis=-1, keepdims=True) + eps_norm)
    normed = center * scaled
    return (normed * gain_vec + offset_vec, normed, scaled)


def normalize_back(upstream, normed, scaled, gain_vec):
    weighted = upstream * gain_vec
    return scaled * (
        weighted
        - jnp.mean(weighted, axis=-1, keepdims=True)
        - normed * jnp.mean(weighted * normed, axis=-1, keepdims=True)
    )


def mm(a, b):
    return jnp.dot(a, b, preferred_element_type=f32)


def mm_t(a, b):
    return lax.dot_general(a, b, contract_cols, preferred_element_type=f32)


def mm_rows(a, b):
    return lax.dot_general(a, b, contract_rows, preferred_element_type=f32)


class Group:
    def __init__(self, name, size):
        self.name, self.size = name, size

    def swap(self, piece, offset):
        return lax.ppermute(piece, self.name, [(i, i ^ offset) for i in range(self.size)])


def xor_order(arr, axis, index, count):
    size = arr.shape[axis]
    bit = 1
    while bit < count:
        wide = arr.reshape(
            arr.shape[:axis] + (count // (2 * bit), 2, bit * size // count) + arr.shape[axis + 1 :]
        )
        flipped = jnp.flip(wide, axis=axis + 1)
        arr = jnp.where((index // bit) % 2 == 1, flipped, wide).reshape(arr.shape)
        bit *= 2
    return arr


def on_device(mesh_sizes, *arrays):
    (
        hidden_in,
        out_cotangent,
        qkv_weight,
        query_value_bias,
        attn_out_weight,
        up_weight,
        up_bias,
        down_weight,
        block_bias,
        norm_gain,
        norm_shift,
    ) = arrays
    fsdp = Group("fsdp", mesh_sizes[0])
    tensor = Group("tensor", mesh_sizes[1])
    own_f = lax.axis_index("fsdp")
    own_t = lax.axis_index("tensor")
    chips = tensor.size // 2
    own_p = (own_t % 2) * chips + own_t // 2
    layer_count, own_width, heads, wide_head = qkv_weight.shape
    head_dim = wide_head // 3
    rows, width = hidden_in.shape
    block_rows = rows // tensor.size
    half = rows // 2
    hidden = up_weight.shape[2]
    mix = heads * head_dim

    def to_rel(arr):
        arr = arr.reshape(chips, 2, block_rows, width).swapaxes(0, 1).reshape(rows, width)
        arr = xor_order(arr, 0, own_p, tensor.size)
        return xor_order(arr, 1, own_f, fsdp.size)

    def to_abs(arr):
        arr = xor_order(arr, 1, own_f, fsdp.size)
        arr = xor_order(arr, 0, own_p, tensor.size)
        return arr.reshape(2, chips, block_rows, width).swapaxes(0, 1).reshape(rows, width)

    def reduce_rows(first, second_low):
        got = tensor.swap(second_low, 1)
        partial = first + got.astype(f32)
        low = partial.astype(bf16)
        total = partial[:block_rows]
        others = [
            tensor.swap(low[c * block_rows : (c + 1) * block_rows], 2 * c) for c in range(1, chips)
        ]
        for other in others:
            total = total + other.astype(f32)
        return total

    def reduce_full(partial_sum):
        return reduce_rows(partial_sum[:half], partial_sum[half:].astype(bf16))

    def spread(block):
        pieces = [block] + [tensor.swap(block, 2 * c) for c in range(1, chips)]
        first = jnp.concatenate(pieces, axis=0)
        return jnp.concatenate([first, tensor.swap(first, 1)], axis=0)

    def gather_f(shard, axis):
        pieces = [shard] + [fsdp.swap(shard, o) for o in range(1, fsdp.size)]
        return jnp.concatenate(pieces, axis=axis)

    def scatter_f(grad, axis):
        size = grad.shape[axis] // fsdp.size
        low = grad.astype(bf16)
        total = lax.slice_in_dim(grad, 0, size, axis=axis)
        for o in range(1, fsdp.size):
            piece = lax.slice_in_dim(low, o * size, (o + 1) * size, axis=axis)
            total = total + fsdp.swap(piece, o).astype(f32)
        return total

    small = jnp.concatenate(
        [
            block_bias.reshape(-1),
            norm_gain.reshape(-1),
            norm_shift.reshape(-1),
            query_value_bias.reshape(-1),
            up_bias.reshape(-1),
        ]
    )
    small_len = small.shape[0]
    pad = (-small_len) % 128
    small = jnp.pad(small, (0, pad)).reshape(-1, 128)
    small_all = jnp.stack([small] + [fsdp.swap(small, o) for o in range(1, fsdp.size)])
    small_all = small_all.reshape(fsdp.size, -1)[:, :small_len].astype(f32)
    n_norm = layer_count * 2 * own_width

    def feature_params(start):
        part = small_all[:, start : start + n_norm].reshape(
            fsdp.size, layer_count, 2, own_width
        )
        return part.transpose(1, 2, 0, 3).reshape(layer_count, 2, width)

    bias_block = feature_params(0)
    gains = feature_params(n_norm)
    offsets = feature_params(2 * n_norm)
    n_qv = query_value_bias.size
    qv_part = xor_order(
        small_all[:, 3 * n_norm : 3 * n_norm + n_qv], 0, own_f, fsdp.size
    ).reshape(fsdp.size, layer_count, heads, -1)
    bias_qv = qv_part.transpose(1, 2, 0, 3).reshape(layer_count, heads, 2 * head_dim)
    up_part = xor_order(small_all[:, 3 * n_norm + n_qv :], 0, own_f, fsdp.size).reshape(
        fsdp.size, layer_count, -1
    )
    bias_up = up_part.transpose(1, 0, 2).reshape(layer_count, hidden)

    def mixed_shard(weight):
        return (
            weight.reshape(own_width, heads, 3, head_dim)
            .transpose(0, 2, 1, 3)
            .reshape(own_width, 3 * mix)
        )

    gathered = []
    token = small_all
    for layer in range(layer_count):
        qkv_s, out_s, up_s, down_s = (
            mixed_shard(qkv_weight[layer]),
            attn_out_weight[layer].reshape(mix, own_width),
            up_weight[layer],
            down_weight[layer],
        )
        if layer == 0:
            w_qkv = gather_f(qkv_s, 0)
            out_s, up_s, down_s, w_qkv, token = lax.optimization_barrier(
                (out_s, up_s, down_s, w_qkv, token)
            )
        else:
            qkv_s, out_s, up_s, down_s, token = lax.optimization_barrier(
                (qkv_s, out_s, up_s, down_s, token)
            )
            w_qkv = gather_f(qkv_s, 0)
        w_out = gather_f(out_s, 1)
        w_up = gather_f(up_s, 0)
        w_down = gather_f(down_s, 1)
        token = w_down[:1]
        gathered.append((w_qkv, w_out, w_up, w_down))

    def heads_of(flat):
        return flat.reshape(rows // SEQ, SEQ, heads, head_dim)

    scale_factor = head_dim**-0.5
    low_full = to_rel(hidden_in)
    cot = to_rel(out_cotangent)[:block_rows]
    stream = low_full[:block_rows].astype(f32)
    stores = []
    for layer in range(layer_count):
        w_qkv, w_out, w_up, w_down = gathered[layer]
        projected = mm(low_full, w_qkv)
        query = heads_of(
            (projected[:, :mix] + bias_qv[layer, :, :head_dim].reshape(1, mix)).astype(bf16)
        )
        key = heads_of(projected[:, mix : 2 * mix].astype(bf16))
        value = heads_of(
            (projected[:, 2 * mix :] + bias_qv[layer, :, head_dim:].reshape(1, mix)).astype(bf16)
        )
        scores = jnp.einsum("bqhd,bkhd->bhqk", query, key, preferred_element_type=f32)
        scores = scores * scale_factor
        row_max = jnp.max(scores, axis=-1, keepdims=True)
        logsum = row_max + jnp.log(jnp.sum(jnp.exp(scores - row_max), axis=-1, keepdims=True))
        probs = jnp.exp(scores - logsum).astype(bf16)
        context = jnp.einsum("bhqk,bkhd->bqhd", probs, value, preferred_element_type=f32)
        context = context.astype(bf16).reshape(rows, mix)
        summed_one = stream + reduce_full(mm(context, w_out)) + bias_block[layer, 0]
        first, normed_one, scale_one = normalize(summed_one, gains[layer, 0], offsets[layer, 0])
        low_norm = spread(first.astype(bf16))
        pre_act = mm(low_norm, w_up) + bias_up[layer]
        activated = (pre_act * gelu_both(pre_act)).astype(bf16)
        summed_two = first + reduce_full(mm(activated, w_down)) + bias_block[layer, 1]
        stream, normed_two, scale_two = normalize(summed_two, gains[layer, 1], offsets[layer, 1])
        stores.append(
            (
                low_full,
                query,
                key,
                value,
                logsum,
                context,
                normed_one,
                scale_one,
                low_norm,
                pre_act,
                activated,
                normed_two,
                scale_two,
            )
        )
        low_full = spread(stream.astype(bf16))
    activations = to_abs(low_full.astype(f32))

    back = cot
    results = [None] * layer_count
    vectors = [None] * layer_count
    for layer in reversed(range(layer_count)):
        w_qkv, w_out, w_up, w_down = gathered[layer]
        (
            low_in,
            query,
            key,
            value,
            logsum,
            context,
            normed_one,
            scale_one,
            low_norm,
            pre_act,
            activated,
            normed_two,
            scale_two,
        ) = stores[layer]
        grad_two = normalize_back(back, normed_two, scale_two, gains[layer, 1])
        low_two = spread(grad_two.astype(bf16))
        slope = gelu_both(pre_act) + pre_act * inv_root_two_pi * jnp.exp(-0.5 * pre_act * pre_act)
        grad_pre = mm_t(low_two, w_down) * slope
        low_pre = grad_pre.astype(bf16)
        grad_first = grad_two + reduce_full(mm_t(low_pre, w_up))
        grad_down = scatter_f(mm_rows(activated, low_two), 1)
        grad_up = scatter_f(mm_rows(low_norm, low_pre), 0)
        grad_up_bias = jnp.sum(grad_pre, axis=0)
        grad_one = normalize_back(grad_first, normed_one, scale_one, gains[layer, 0])
        low_one = spread(grad_one.astype(bf16))
        grad_context = heads_of(mm_t(low_one, w_out).astype(bf16))
        scores = jnp.einsum("bqhd,bkhd->bhqk", query, key, preferred_element_type=f32)
        probs = jnp.exp(scores * scale_factor - logsum)
        grad_value = jnp.einsum(
            "bhqk,bqhd->bkhd", probs.astype(bf16), grad_context, preferred_element_type=f32
        )
        grad_probs = jnp.einsum(
            "bqhd,bkhd->bhqk", grad_context, value, preferred_element_type=f32
        )
        inner = jnp.sum(probs * grad_probs, axis=-1, keepdims=True)
        grad_scores = (probs * (grad_probs - inner)).astype(bf16)
        grad_query = (
            jnp.einsum("bhqk,bkhd->bqhd", grad_scores, key, preferred_element_type=f32)
            * scale_factor
        )
        grad_key = (
            jnp.einsum("bhqk,bqhd->bkhd", grad_scores, query, preferred_element_type=f32)
            * scale_factor
        )
        grad_query, grad_key, grad_value = (
            part.reshape(rows, mix) for part in (grad_query, grad_key, grad_value)
        )
        low_mixed = jnp.concatenate([grad_query, grad_key, grad_value], axis=1).astype(bf16)
        back_next = grad_one + reduce_full(mm_t(low_mixed, w_qkv))
        grad_out = scatter_f(mm_rows(context, low_one), 1)
        grad_qkv = scatter_f(mm_rows(low_in, low_mixed), 0)
        grad_qkv = (
            grad_qkv.reshape(own_width, 3, heads, head_dim)
            .transpose(0, 2, 1, 3)
            .reshape(own_width, heads, wide_head)
        )
        grad_q = jnp.sum(grad_query, axis=0).reshape(heads, head_dim)
        grad_v = jnp.sum(grad_value, axis=0).reshape(heads, head_dim)
        vector = jnp.stack(
            [
                jnp.sum(grad_one, axis=0),
                jnp.sum(grad_two, axis=0),
                jnp.sum(grad_first * normed_one, axis=0),
                jnp.sum(back * normed_two, axis=0),
                jnp.sum(grad_first, axis=0),
                jnp.sum(back, axis=0),
            ]
        )
        vectors[layer] = scatter_f(vector, 1)
        local = jnp.concatenate([grad_q, grad_v], axis=-1).reshape(heads, fsdp.size, -1)
        local = local.transpose(1, 0, 2).reshape(fsdp.size, -1)
        local = jnp.concatenate([local, grad_up_bias.reshape(fsdp.size, -1)], axis=1)
        local = xor_order(local, 0, own_f, fsdp.size)
        local = scatter_f(local, 0)[0]
        n_qv_own = heads * 2 * head_dim // fsdp.size
        results[layer] = (
            grad_qkv,
            local[:n_qv_own].reshape(heads, -1),
            grad_out.reshape(heads, head_dim, own_width),
            grad_up,
            local[n_qv_own:],
            grad_down,
        )
        back = back_next

    input_grad = to_abs(spread(back.astype(bf16)).astype(f32))
    vec = jnp.concatenate(vectors, axis=0)
    low_vec = vec.astype(bf16)
    total = vec
    for o in range(1, tensor.size):
        total = total + tensor.swap(low_vec, o).astype(f32)
    total = total.reshape(layer_count, 3, 2, own_width)
    outputs = [jnp.stack([member[i] for member in results]) for i in range(6)]
    return (
        activations,
        input_grad,
        *outputs,
        total[:, 0],
        total[:, 1],
        total[:, 2],
    )


def solution(mesh):
    in_specs = (
        P("fsdp", None),
        P("fsdp", None),
        P(None, "fsdp", "tensor", None),
        P(None, "tensor", "fsdp"),
        P(None, "tensor", None, "fsdp"),
        P(None, "fsdp", "tensor"),
        P(None, ("tensor", "fsdp")),
        P(None, "tensor", "fsdp"),
        P(None, None, "fsdp"),
        P(None, None, "fsdp"),
        P(None, None, "fsdp"),
    )
    out_specs = in_specs
    sizes = (mesh.shape["fsdp"], mesh.shape["tensor"])

    def body(*arrays):
        return on_device(sizes, *arrays)

    return jax.shard_map(
        body, mesh=mesh, in_specs=in_specs, out_specs=out_specs, check_vma=False
    )
```

```python
import functools

import jax
import jax.numpy as jnp
from jax import lax
from jax.experimental import pallas as pl
from jax.experimental.pallas import tpu as pltpu
from jax.sharding import PartitionSpec as P

SEQ = 512

eps_norm = 1e-05
root_half = 0.7071067811865476
inv_root_two_pi = 0.3989422804014327
f32 = jnp.float32
bf16 = jnp.bfloat16


def mm(a, b):
    return jnp.dot(a, b, preferred_element_type=f32)


def mm_t(a, b):
    return lax.dot_general(a, b, (((1,), (1,)), ((), ())), preferred_element_type=f32)


def mm_rows(a, b):
    return lax.dot_general(a, b, (((0,), (0,)), ((), ())), preferred_element_type=f32)


def shape(dims, dtype):
    return jax.ShapeDtypeStruct(dims, dtype)


def call(body, outs, args, flops=1_000_000, name=None, **kwargs):
    moved = sum(a.size * a.dtype.itemsize for a in args) + sum(
        o.size * o.dtype.itemsize for o in outs
    )
    return pl.pallas_call(
        body,
        out_shape=outs,
        name=name,
        cost_estimate=pl.CostEstimate(flops=flops, bytes_accessed=moved, transcendentals=0),
        **kwargs,
    )(*args)


def normalize_rows(summed, gain, shift):
    center = summed - jnp.mean(summed, axis=-1, keepdims=True)
    scale = lax.rsqrt(jnp.mean(center * center, axis=-1, keepdims=True) + eps_norm)
    normed = center * scale
    return normed * gain + shift, normed, scale


def normalize_back_rows(upstream, normed, scale, gain):
    weighted = upstream * gain
    return scale * (
        weighted
        - jnp.mean(weighted, axis=-1, keepdims=True)
        - normed * jnp.mean(weighted * normed, axis=-1, keepdims=True)
    )


def to_rel_kernel(count_f, count_t, index, hidden, cot, first, second, own_cot):
    own_f, own_t = index[0], index[1]
    rows, width = hidden.shape
    size, wide = rows // count_t, width // count_f
    chips = count_t // 2
    for p in range(count_t):
        offset = 2 * (p % chips) + p // chips
        start = pl.multiple_of((own_t ^ offset) * size, size)
        target = first if p < chips else second
        at = (p % chips) * size
        for j in range(count_f):
            column = pl.multiple_of((own_f ^ j) * wide, wide)
            target[at : at + size, j * wide : (j + 1) * wide] = hidden[
                pl.ds(start, size), pl.ds(column, wide)
            ]
    start = pl.multiple_of(own_t * size, size)
    for j in range(count_f):
        column = pl.multiple_of((own_f ^ j) * wide, wide)
        own_cot[:, j * wide : (j + 1) * wide] = cot[pl.ds(start, size), pl.ds(column, wide)]


def to_abs_kernel(count_f, count_t, index, first, second, out):
    own_f, own_t = index[0], index[1]
    rows, width = out.shape
    size, wide = rows // count_t, width // count_f
    chips = count_t // 2
    for p in range(count_t):
        offset = 2 * (p % chips) + p // chips
        start = pl.multiple_of((own_t ^ offset) * size, size)
        source = first if p < chips else second
        at = (p % chips) * size
        for j in range(count_f):
            column = pl.multiple_of((own_f ^ j) * wide, wide)
            out[pl.ds(start, size), pl.ds(column, wide)] = source[
                at : at + size, j * wide : (j + 1) * wide
            ].astype(f32)


def store_parts(part, first, second, j, wide):
    half = part.shape[0] // 2
    first[:, j * wide : (j + 1) * wide] = part[:half]
    second[:, j * wide : (j + 1) * wide] = part[half:].astype(bf16)


def joined(first, second, j, wide):
    at = slice(j * wide, (j + 1) * wide)
    return jnp.concatenate([first[:, at], second[:, at]], axis=0)


def attend_kernel(count, heads, *refs):
    first, second = refs[:2]
    weights = refs[2 : 2 + count]
    bias, query_o, key_o, value_o, context_o, logsum_o, part_a, part_b = refs[2 + count :]
    wide = first.shape[1] // count
    mix = query_o.shape[1]
    head = mix // heads
    projected = None
    for j in range(count):
        term = mm_t(joined(first, second, j, wide), weights[j][: 3 * mix, :])
        projected = term if projected is None else projected + term
    query_o[...] = (projected[:, :mix] + bias[0:1, :]).astype(bf16)
    key_o[...] = projected[:, mix : 2 * mix].astype(bf16)
    value_o[...] = (projected[:, 2 * mix :] + bias[1:2, :]).astype(bf16)
    for s in range(query_o.shape[0] // SEQ):
        at = slice(s * SEQ, (s + 1) * SEQ)
        for h in range(heads):
            cols = slice(h * head, (h + 1) * head)
            scores = mm_t(query_o[at, cols], key_o[at, cols]) * (head**-0.5)
            row_max = jnp.max(scores, axis=-1, keepdims=True)
            grown = jnp.exp(scores - row_max)
            total = jnp.sum(grown, axis=-1, keepdims=True)
            probs = (grown * (1.0 / total)).astype(bf16)
            context_o[at, cols] = mm(probs, value_o[at, cols]).astype(bf16)
            logsum_o[at, h : h + 1] = row_max + jnp.log(total)
    context = context_o[...]
    for j in range(count):
        store_parts(mm(context, weights[j][3 * mix : 4 * mix, :]), part_a, part_b, j, wide)


def mlp_kernel(count, *refs):
    first, second = refs[:2]
    weights = refs[2 : 2 + count]
    bias, active_o, slope_o, part_a, part_b = refs[2 + count :]
    wide = first.shape[1] // count
    hidden = active_o.shape[1]
    for c in range(hidden // wide):
        cols = slice(c * wide, (c + 1) * wide)
        pre_act = None
        for j in range(count):
            term = mm(joined(first, second, j, wide), weights[j][cols, :])
            pre_act = term if pre_act is None else pre_act + term
        pre_act = pre_act + bias[0:1, cols]
        gate = 0.5 * (1.0 + lax.erf(pre_act * root_half))
        active_o[:, cols] = (pre_act * gate).astype(bf16)
        slope_o[:, cols] = gate + pre_act * inv_root_two_pi * jnp.exp(-0.5 * pre_act * pre_act)
    active = active_o[...]
    for j in range(count):
        store_parts(mm(active, weights[j][hidden:, :]), part_a, part_b, j, wide)


def mlp_back_kernel(count, *refs):
    first, second = refs[:2]
    weights = refs[2 : 2 + count]
    slope, low_pre_o, bias_o, part_a, part_b = refs[2 + count :]
    wide = first.shape[1] // count
    hidden = slope.shape[1]
    grad = None
    for j in range(count):
        term = mm_t(joined(first, second, j, wide), weights[j][hidden:, :])
        grad = term if grad is None else grad + term
    grad = grad * slope[...]
    bias_o[...] = jnp.sum(grad, axis=0, keepdims=True)
    low_pre_o[...] = grad.astype(bf16)
    for j in range(count):
        part = None
        for c in range(hidden // wide):
            cols = slice(c * wide, (c + 1) * wide)
            term = mm_t(low_pre_o[:, cols], weights[j][cols, :])
            part = term if part is None else part + term
        store_parts(part, part_a, part_b, j, wide)


def mlp_grad_kernel(count, first, second, norm_a, norm_b, active, low_pre, *outs):
    wide = first.shape[1] // count
    hidden = active.shape[1]
    act, pre = active[...], low_pre[...]
    for j in range(count):
        out = outs[j]
        out[hidden:, :] = mm_rows(act, joined(first, second, j, wide)).astype(out.dtype)
        norm = joined(norm_a, norm_b, j, wide)
        up = mm_rows(norm, pre)
        for c in range(hidden // wide):
            cols = slice(c * wide, (c + 1) * wide)
            out[cols, :] = up[:, cols].astype(out.dtype)


def attend_back_kernel(count, heads, *refs):
    first, second = refs[:2]
    weights = refs[2 : 2 + count]
    query, key, value, logsum, mixed_o, sums_o, part_a, part_b = refs[2 + count :]
    wide = first.shape[1] // count
    mix = query.shape[1]
    head = mix // heads
    factor = head**-0.5
    grad = None
    for j in range(count):
        term = mm_t(joined(first, second, j, wide), weights[j][3 * mix : 4 * mix, :])
        grad = term if grad is None else grad + term
    grad = grad.astype(bf16)
    sums_o[...] = jnp.zeros_like(sums_o)
    for s in range(query.shape[0] // SEQ):
        at = slice(s * SEQ, (s + 1) * SEQ)
        for h in range(heads):
            cols = slice(h * head, (h + 1) * head)
            q, k, v, g = query[at, cols], key[at, cols], value[at, cols], grad[at, cols]
            probs = jnp.exp(mm_t(q, k) * factor - logsum[at, h : h + 1])
            grad_v = mm_rows(probs.astype(bf16), g)
            grad_p = mm_t(g, v)
            inner = jnp.sum(probs * grad_p, axis=-1, keepdims=True)
            grad_s = (probs * (grad_p - inner)).astype(bf16)
            grad_q = mm(grad_s, k) * factor
            grad_k = mm_rows(grad_s, q) * factor
            mixed_o[at, h * head : (h + 1) * head] = grad_q.astype(bf16)
            mixed_o[at, mix + h * head : mix + (h + 1) * head] = grad_k.astype(bf16)
            mixed_o[at, 2 * mix + h * head : 2 * mix + (h + 1) * head] = grad_v.astype(bf16)
            sums_o[0:1, cols] += jnp.sum(grad_q, axis=0, keepdims=True)
            sums_o[1:2, cols] += jnp.sum(grad_v, axis=0, keepdims=True)
    mixed = mixed_o[...]
    for j in range(count):
        store_parts(mm(mixed, weights[j][: 3 * mix, :]), part_a, part_b, j, wide)


def attend_grad_kernel(count, first, second, in_a, in_b, context, mixed, *outs):
    wide = first.shape[1] // count
    three = mixed.shape[1]
    ctx, mix = context[...], mixed[...]
    for j in range(count):
        out = outs[j]
        out[:three, :] = mm_rows(mix, joined(in_a, in_b, j, wide)).astype(out.dtype)
        out[three:, :] = mm_rows(ctx, joined(first, second, j, wide)).astype(out.dtype)


def add_half_kernel(first, got, own, *lows):
    size = own.shape[0]
    own[...] = first[:size] + got[:size].astype(f32)
    for c, low in enumerate(lows):
        at = slice((c + 1) * size, (c + 2) * size)
        low[...] = (first[at] + got[at].astype(f32)).astype(bf16)


def cat_kernel(*refs):
    out = refs[-1]
    size = refs[0].shape[0]
    for c, ref in enumerate(refs[:-1]):
        out[c * size : (c + 1) * size, :] = ref[...]


def total_of(refs):
    total = refs[0][...]
    for ref in refs[1:]:
        total = total + ref[...].astype(f32)
    return total


def row_of(smalls, row):
    return jnp.concatenate([s[row : row + 1, :].astype(f32) for s in smalls], axis=1)


def norm_kernel(count, chips, base, rows_at, *refs):
    parts = refs[:chips]
    stream = refs[chips]
    smalls = refs[chips + 1 : chips + 1 + count]
    out_o, low_o, normed_o, scale_o = refs[chips + 1 + count :]
    views = [s.at[base:, :] for s in smalls]
    bias_at, gain_at, shift_at = rows_at
    summed = stream[...].astype(f32) + total_of(parts) + row_of(views, bias_at)
    out, normed, scale = normalize_rows(summed, row_of(views, gain_at), row_of(views, shift_at))
    out_o[...] = out
    low_o[...] = out.astype(bf16)
    normed_o[...] = normed
    scale_o[...] = scale


def norm_back_kernel(count, chips, base, gain_at, *refs):
    parts = refs[:chips]
    residual, normed_r, scale_r = refs[chips : chips + 3]
    smalls = refs[chips + 3 : chips + 3 + count]
    grad_o, low_o, sums_o = refs[chips + 3 + count :]
    views = [s.at[base:, :] for s in smalls]
    back = residual[...]
    if chips:
        back = back + total_of(parts)
    normed = normed_r[...]
    grad = normalize_back_rows(back, normed, scale_r[...], row_of(views, gain_at))
    grad_o[...] = grad
    low_o[...] = grad.astype(bf16)
    sums_o[0:1, :] = jnp.sum(grad, axis=0, keepdims=True)
    sums_o[1:2, :] = jnp.sum(back * normed, axis=0, keepdims=True)
    sums_o[2:3, :] = jnp.sum(back, axis=0, keepdims=True)


def last_kernel(*refs):
    refs[-1][...] = (refs[0][...] + total_of(refs[1:-1])).astype(bf16)


class Group:
    def __init__(self, name, size):
        self.name, self.size = name, size

    def swap(self, piece, offset):
        return lax.ppermute(piece, self.name, [(i, i ^ offset) for i in range(self.size)])


def reorder(rel, own):
    count = rel.shape[0]
    k = jnp.arange(count, dtype=jnp.int32)
    pick = (k[:, None] ^ own) == k[None, :]
    return jnp.sum(jnp.where(pick[:, :, None], rel[None], 0), axis=1)


def on_device(mesh_sizes, *arrays):
    (
        hidden_in,
        out_cotangent,
        qkv_weight,
        query_value_bias,
        attn_out_weight,
        up_weight,
        up_bias,
        down_weight,
        block_bias,
        norm_gain,
        norm_shift,
    ) = arrays
    fsdp = Group("fsdp", mesh_sizes[0])
    tensor = Group("tensor", mesh_sizes[1])
    own_f = lax.axis_index("fsdp")
    own_t = lax.axis_index("tensor")
    count = fsdp.size
    chips = tensor.size // 2
    layers, wide, heads, wide_head = qkv_weight.shape
    head = wide_head // 3
    rows, width = hidden_in.shape
    size = rows // tensor.size
    half = rows // 2
    hidden = up_weight.shape[2]
    mix = heads * head
    index = jnp.stack([own_f, own_t]).astype(jnp.int32)

    half_low = shape((half, width), bf16)
    half_wide = shape((half, width), f32)
    own_low = shape((size, width), bf16)
    own_wide = shape((size, width), f32)
    one_col = shape((size, 1), f32)

    smem = pl.BlockSpec(memory_space=pltpu.SMEM)
    vmem = pl.BlockSpec(memory_space=pltpu.VMEM)

    def reduce_rows(part_a, part_b):
        got = tensor.swap(part_b, 1)
        pieces = call(
            add_half_kernel, (own_wide,) + (own_low,) * (chips - 1), (part_a, got), name="add_half"
        )
        return [pieces[0]] + [tensor.swap(pieces[c], 2 * c) for c in range(1, chips)]

    def spread(block):
        pieces = [block] + [tensor.swap(block, 2 * c) for c in range(1, chips)]
        first = call(cat_kernel, (half_low,), pieces, name="cat")[0]
        return first, tensor.swap(first, 1)

    def gather_f(shard):
        return [shard] + [fsdp.swap(shard, o) for o in range(1, count)]

    def row(vec):
        return jnp.pad(vec.reshape(1, -1), ((0, 0), (0, wide - vec.size)))

    small = jnp.concatenate(
        [
            block_bias.reshape(2 * layers, wide),
            norm_gain.reshape(2 * layers, wide),
            norm_shift.reshape(2 * layers, wide),
            row(query_value_bias),
            row(up_bias),
        ]
    )
    n_small = small.shape[0]
    small = jnp.pad(small, ((0, (-n_small) % 16), (0, 0)))
    base = 4 * mix
    qv_row, up_row = base + 6 * layers, base + 6 * layers + 1

    qkv_t = (
        qkv_weight.reshape(layers, wide, heads, 3, head)
        .transpose(0, 3, 2, 4, 1)
        .reshape(layers, 3 * mix, wide)
    )
    out_rows = attn_out_weight.reshape(layers, mix, wide)
    chunks = hidden // wide
    up_rows = (
        up_weight.reshape(layers, wide, chunks, wide)
        .transpose(0, 2, 1, 3)
        .reshape(layers, hidden, wide)
    )
    attend_packs, mlp_packs = [], []
    token = None
    for layer in range(layers):
        attend_src = [qkv_t[layer], out_rows[layer]] + ([small] if layer == 0 else [])
        attend_src = jnp.concatenate(attend_src)
        if token is not None:
            attend_src, token = lax.optimization_barrier((attend_src, token))
        pack = gather_f(attend_src)
        attend_packs.append(pack)
        token = pack[-1]
        mlp_src = jnp.concatenate([up_rows[layer], down_weight[layer]])
        mlp_src, token = lax.optimization_barrier((mlp_src, token))
        pack = gather_f(mlp_src)
        mlp_packs.append(pack)
        token = pack[-1]
    smalls = attend_packs[0]

    qv_rel = jnp.stack([s[qv_row, : query_value_bias.size] for s in smalls]).astype(f32)
    qv_abs = reorder(qv_rel, own_f).reshape(count, layers, heads, -1).transpose(1, 2, 0, 3)
    qv_abs = qv_abs.reshape(layers, heads, 2, head).transpose(0, 2, 1, 3).reshape(layers, 2, mix)
    up_rel = jnp.stack([s[up_row, : up_bias.size] for s in smalls]).astype(f32)
    up_abs = reorder(up_rel, own_f).reshape(count, layers, -1).transpose(1, 0, 2)
    up_abs = up_abs.reshape(layers, 1, hidden)

    first, second, cot = call(
        functools.partial(to_rel_kernel, count, tensor.size),
        (half_low, half_low, own_wide),
        (index, hidden_in, out_cotangent),
        in_specs=[smem, vmem, vmem],
        name="to_rel",
    )
    to_abs = functools.partial(to_abs_kernel, count, tensor.size)

    def absolute(pair):
        return call(
            to_abs,
            (shape((rows, width), f32),),
            (index, *pair),
            in_specs=[smem, vmem, vmem],
            name="to_abs",
        )[0]

    parts_shape = (half_wide, half_low)
    stream = first[:size]
    stores = []
    for layer in range(layers):
        outs = (shape((rows, mix), bf16),) * 4 + (shape((rows, heads), f32),) + parts_shape
        query, key, value, context, logsum, *parts = call(
            functools.partial(attend_kernel, count, heads),
            outs,
            (first, second, *attend_packs[layer], qv_abs[layer]),
            flops=8 * rows * width * mix + 4 * rows * SEQ * mix,
            name="attend",
        )
        rows_at = (2 * layer, 2 * layers + 2 * layer, 4 * layers + 2 * layer)
        first_norm, low, normed_one, scale_one = call(
            functools.partial(norm_kernel, count, chips, base, rows_at),
            (own_wide, own_low, own_wide, one_col),
            (*reduce_rows(*parts), stream, *smalls),
            name="norm",
        )
        norm_a, norm_b = spread(low)
        active, slope, *parts = call(
            functools.partial(mlp_kernel, count),
            (shape((rows, hidden), bf16), shape((rows, hidden), f32)) + parts_shape,
            (norm_a, norm_b, *mlp_packs[layer], up_abs[layer]),
            flops=4 * rows * width * hidden,
            name="mlp",
        )
        rows_at = tuple(r + 1 for r in rows_at)
        stream, low, normed_two, scale_two = call(
            functools.partial(norm_kernel, count, chips, base, rows_at),
            (own_wide, own_low, own_wide, one_col),
            (*reduce_rows(*parts), first_norm, *smalls),
            name="norm",
        )
        stores.append(
            (
                first,
                second,
                query,
                key,
                value,
                logsum,
                context,
                normed_one,
                scale_one,
                norm_a,
                norm_b,
                active,
                slope,
                normed_two,
                scale_two,
            )
        )
        first, second = spread(low)
    activations = absolute((first, second))

    sums_shape = shape((3, width), f32)
    back_parts, residual = [], cot
    exchanged = {}
    vectors = [None] * (2 * layers)
    local_sums = []
    for layer in reversed(range(layers)):
        (
            in_a,
            in_b,
            query,
            key,
            value,
            logsum,
            context,
            normed_one,
            scale_one,
            norm_a,
            norm_b,
            active,
            slope,
            normed_two,
            scale_two,
        ) = stores[layer]
        gain_at = 2 * layers + 2 * layer
        grad_two, low, vectors[2 * layer + 1] = call(
            functools.partial(norm_back_kernel, count, len(back_parts), base, gain_at + 1),
            (own_wide, own_low, sums_shape),
            (*back_parts, residual, normed_two, scale_two, *smalls),
            name="norm_back",
        )
        two_a, two_b = spread(low)
        low_pre, up_sum, *parts = call(
            functools.partial(mlp_back_kernel, count),
            (shape((rows, hidden), bf16), shape((1, hidden), f32)) + parts_shape,
            (two_a, two_b, *mlp_packs[layer], slope),
            flops=4 * rows * width * hidden,
            name="mlp_back",
        )
        back_parts = reduce_rows(*parts)
        grads = call(
            functools.partial(mlp_grad_kernel, count),
            (shape((2 * hidden, wide), f32),) + (shape((2 * hidden, wide), bf16),) * (count - 1),
            (two_a, two_b, norm_a, norm_b, active, low_pre),
            flops=4 * rows * width * hidden,
            name="mlp_grad",
        )
        exchanged["mlp", layer] = [grads[0]] + [
            fsdp.swap(grads[o], o) for o in range(1, count)
        ]
        grad_one, low, vectors[2 * layer] = call(
            functools.partial(norm_back_kernel, count, chips, base, gain_at),
            (own_wide, own_low, sums_shape),
            (*back_parts, grad_two, normed_one, scale_one, *smalls),
            name="norm_back",
        )
        if layer == 0:
            vector = jnp.concatenate(vectors)
            bit = 1
            while bit < tensor.size:
                vector = vector + tensor.swap(vector, bit)
                bit *= 2
        one_a, one_b = spread(low)
        mixed, qv_sum, *parts = call(
            functools.partial(attend_back_kernel, count, heads),
            (shape((rows, 3 * mix), bf16), shape((2, mix), f32)) + parts_shape,
            (one_a, one_b, *attend_packs[layer], query, key, value, logsum),
            flops=8 * rows * width * mix + 10 * rows * SEQ * mix,
            name="attend_back",
        )
        back_parts = reduce_rows(*parts)
        residual = grad_one
        grads = call(
            functools.partial(attend_grad_kernel, count),
            (shape((4 * mix, wide), f32),) + (shape((4 * mix, wide), bf16),) * (count - 1),
            (one_a, one_b, in_a, in_b, context, mixed),
            flops=8 * rows * width * mix,
            name="attend_grad",
        )
        local_sums.append((layer, up_sum, qv_sum))
        if layer == 0:
            pieces = []
            for _, up_sum, qv_sum in sorted(local_sums, key=lambda item: item[0]):
                by_head = qv_sum.reshape(2, heads, head).transpose(1, 0, 2)
                by_block = by_head.reshape(heads, count, -1).transpose(1, 0, 2)
                pieces.append(by_block.reshape(count, -1))
            n_qv = pieces[0].shape[1]
            for _, up_sum, qv_sum in sorted(local_sums, key=lambda item: item[0]):
                pieces.append(up_sum.reshape(count, -1))
            local = reorder(jnp.concatenate(pieces, axis=1), own_f)
            local = jnp.pad(local, ((0, 0), (0, (-local.shape[1]) % wide)))
            local = local.reshape(count, -1, wide)
            feats = vector.reshape(6 * layers, count, wide).transpose(1, 0, 2)
            rest = jnp.concatenate([feats, local], axis=1)
            rest = jnp.pad(rest, ((0, 0), (0, (-rest.shape[1]) % 16), (0, 0)))
            grads = [jnp.concatenate([grads[0], rest[0]])] + [
                jnp.concatenate([grads[o], rest[o].astype(bf16)]) for o in range(1, count)
            ]
        exchanged["attend", layer] = [grads[0]] + [
            fsdp.swap(grads[o], o) for o in range(1, count)
        ]

    back = call(last_kernel, (own_low,), (residual, *back_parts), name="last")[0]
    input_grad = absolute(spread(back))

    def summed(pieces):
        total = pieces[0]
        for piece in pieces[1:]:
            total = total + piece.astype(f32)
        return total

    attend_sums = [summed(exchanged["attend", layer]) for layer in range(layers)]
    mlp_sums = [summed(exchanged["mlp", layer]) for layer in range(layers)]
    small_sum = attend_sums[0][4 * mix :]
    vector = small_sum[: 6 * layers].reshape(layers, 2, 3, wide)
    local = small_sum[6 * layers :].reshape(-1)
    grad_qkv = jnp.stack(
        [
            s[: 3 * mix].reshape(3, heads, head, wide).transpose(3, 1, 0, 2)
            for s in attend_sums
        ]
    ).reshape(qkv_weight.shape)
    grad_out = jnp.stack([s[3 * mix : 4 * mix] for s in attend_sums])
    grad_up = jnp.stack(
        [s[:hidden].reshape(chunks, wide, wide).transpose(1, 0, 2) for s in mlp_sums]
    ).reshape(up_weight.shape)
    grad_down = jnp.stack([s[hidden:] for s in mlp_sums])
    return (
        activations,
        input_grad,
        grad_qkv,
        local[: layers * n_qv].reshape(query_value_bias.shape),
        grad_out.reshape(attn_out_weight.shape),
        grad_up,
        local[layers * n_qv : layers * n_qv + up_bias.size].reshape(up_bias.shape),
        grad_down,
        vector[:, :, 0],
        vector[:, :, 1],
        vector[:, :, 2],
    )


def solution(mesh):
    specs = (
        P("fsdp", None),
        P("fsdp", None),
        P(None, "fsdp", "tensor", None),
        P(None, "tensor", "fsdp"),
        P(None, "tensor", None, "fsdp"),
        P(None, "fsdp", "tensor"),
        P(None, ("tensor", "fsdp")),
        P(None, "tensor", "fsdp"),
        P(None, None, "fsdp"),
        P(None, None, "fsdp"),
        P(None, None, "fsdp"),
    )
    sizes = (mesh.shape["fsdp"], mesh.shape["tensor"])
    return jax.shard_map(
        functools.partial(on_device, sizes),
        mesh=mesh,
        in_specs=specs,
        out_specs=specs,
        check_vma=False,
    )
```
